32 devices in a mesh: dp: 4 (over z), row: 2 (over core), col: 4 (over y, x).
Axes of the slice: x: 2, y: 2, z: 4, core: 2. Of those that a mesh axis runs over, the one named last changes fastest.
Arguments:
- residual_in: float32 [2048, 1024], P('dp', ('row', 'col')), may hold values from -6 to 6
- positions: int32 [2048], P('dp'), may hold values from 0 to 511, as said below
- attn_gain: float32 [2, 1024], P(None, ('row', 'col')), may hold values from 0.1 to 1.9
- query_weight: bfloat16 [2, 1024, 2048], P(None, 'row', 'col'), may hold values from -0.1875 to 0.1875
- key_weight: bfloat16 [2, 1024, 1024], P(None, 'row', 'col'), may hold values from -0.1875 to 0.1875
- value_weight: bfloat16 [2, 1024, 1024], P(None, 'row', 'col'), may hold values from -0.1875 to 0.1875
- query_gain: float32 [2, 128], replicated, may hold values from 0.1 to 1.9
- key_gain: float32 [2, 128], replicated, may hold values from 0.1 to 1.9
- output_weight: bfloat16 [2, 2048, 1024], P(None, 'col', 'row'), may hold values from -1 to 1
- ffn_gain: float32 [2, 1024], P(None, ('row', 'col')), may hold values from 0.1 to 1.9
- gate_weight: bfloat16 [2, 1024, 3072], P(None, 'row', 'col'), may hold values from -0.1875 to 0.1875
- up_weight: bfloat16 [2, 1024, 3072], P(None, 'row', 'col'), may hold values from -0.1875 to 0.1875
- down_weight: bfloat16 [2, 3072, 1024], P(None, 'col', 'row'), may hold values from -0.109375 to 0.109375
- output_grad: float32 [2048, 1024], P('dp', ('row', 'col')), may hold values from -6 to 6
Outputs:
- outputs: float32 [2048, 1024], P('dp', ('row', 'col'))
- input_grad: float32 [2048, 1024], P('dp', ('row', 'col'))
- attn_gain_grad: float32 [2, 1024], P(None, ('row', 'col'))
- query_weight_grad: float32 [2, 1024, 2048], P(None, 'row', 'col')
- key_weight_grad: float32 [2, 1024, 1024], P(None, 'row', 'col')
- value_weight_grad: float32 [2, 1024, 1024], P(None, 'row', 'col')
- query_gain_grad: float32 [2, 128], replicated
- key_gain_grad: float32 [2, 128], replicated
- output_weight_grad: float32 [2, 2048, 1024], P(None, 'col', 'row')
- ffn_gain_grad: float32 [2, 1024], P(None, ('row', 'col'))
- gate_weight_grad: float32 [2, 1024, 3072], P(None, 'row', 'col')
- up_weight_grad: float32 [2, 1024, 3072], P(None, 'row', 'col')
- down_weight_grad: float32 [2, 3072, 1024], P(None, 'col', 'row')
The draws below stay inside these ranges and needn't reach their ends.
Inputs may be any that keep to these rules, and one draw needn't show every extreme that they name: `positions`: within each sequence of 512 tokens, the first position is 0 and each later one is either 0 or one more than the one before.
All inputs are finite; a program needn't handle non-finite values.
Results may differ from the reference program's by a relative error of at most 0.035.
Values may be sent and summed in bfloat16 or wider, within the bound.
A program may use at most 128 MiB of HBM per device.

```python
import jax
import jax.numpy as jnp
from jax import lax

D = 1024
HEADS = 16
KV_HEADS = 8
HEAD_DIM = 128
FF = 3072
LAYERS = 2
SEQ_LEN = 512
TOKENS = 2048


def draw_positions(key, part):
    seq_count = TOKENS // SEQ_LEN
    starts = jax.random.randint(key, (seq_count, SEQ_LEN), 0, 48) == 0
    starts = starts.at[:, 0].set(True)
    starts = starts.at[0, :].set(False)
    starts = starts.at[0, 0].set(True)
    index_row = jnp.arange(SEQ_LEN, dtype=jnp.int32)
    latest = lax.cummax(jnp.where(starts, index_row[None, :], 0), axis=1)
    return (index_row[None, :] - latest).reshape(TOKENS).astype(jnp.int32)


def level_of(own_key, extent, pieces, smallest, high):
    level, own = 1.0, jax.random.fold_in(own_key, 6)
    for dim, parts in pieces:
        steps = jnp.exp(jax.random.uniform(jax.random.fold_in(own, dim), (parts,), jnp.float32, smallest / len(pieces), high / len(pieces)))
        level = level * jnp.repeat(steps, extent[dim] // parts).reshape([-1 if axis == dim else 1 for axis in range(len(extent))])
    return level


def normal_values(rng, extent, spread, limit, pieces=(), kind=jnp.bfloat16):
    loudness = level_of(rng, extent, pieces, -0.22, 0.18) if pieces else 1.0
    values = jax.random.normal(rng, extent, jnp.float32) * spread * loudness
    return jnp.minimum(jnp.maximum(values, -limit), limit).astype(kind)


def setup_inputs(seed: int = 0) -> dict:
    seeds = jax.random.split(jax.random.key(seed), 15)
    return {
        "residual_in": normal_values(seeds[0], (TOKENS, D), 1.0, 6.0, ((0, 4), (1, 8)), jnp.float32),
        "positions": draw_positions(jax.random.fold_in(seeds[14], 71), 0),
        "attn_gain": jnp.clip(1.0 + 0.18 * jax.random.normal(seeds[2], (LAYERS, D), jnp.float32), 0.1, 1.9),
        "query_weight": normal_values(seeds[3], (LAYERS, D, HEADS * HEAD_DIM), D ** -0.5, 0.1875, ((1, 2), (2, 4))),
        "key_weight": normal_values(seeds[4], (LAYERS, D, KV_HEADS * HEAD_DIM), D ** -0.5, 0.1875, ((1, 2), (2, 4))),
        "value_weight": normal_values(seeds[5], (LAYERS, D, KV_HEADS * HEAD_DIM), D ** -0.5, 0.1875, ((1, 2), (2, 4))),
        "query_gain": jnp.clip(1.0 + 0.18 * jax.random.normal(seeds[6], (LAYERS, HEAD_DIM), jnp.float32), 0.1, 1.9),
        "key_gain": jnp.clip(1.0 + 0.18 * jax.random.normal(seeds[7], (LAYERS, HEAD_DIM), jnp.float32), 0.1, 1.9),
        "output_weight": normal_values(seeds[8], (LAYERS, HEADS * HEAD_DIM, D), (HEADS * HEAD_DIM // 64) ** -0.5, 1.0, ((1, 4), (2, 2))),
        "ffn_gain": jnp.clip(1.0 + 0.18 * jax.random.normal(seeds[9], (LAYERS, D), jnp.float32), 0.1, 1.9),
        "gate_weight": normal_values(seeds[10], (LAYERS, D, FF), D ** -0.5, 0.1875, ((1, 2), (2, 4))),
        "up_weight": normal_values(seeds[11], (LAYERS, D, FF), D ** -0.5, 0.1875, ((1, 2), (2, 4))),
        "down_weight": normal_values(seeds[12], (LAYERS, FF, D), FF ** -0.5, 0.109375, ((1, 4), (2, 2))),
        "output_grad": normal_values(seeds[13], (TOKENS, D), 1.0, 6.0, ((0, 4), (1, 8)), jnp.float32),
    }


epsilon = 1e-06
rope_base = 1000000.0
masked_score = -1e+30

def to_bf16(values):
    return lax.optimization_barrier(values.astype(jnp.bfloat16))

def matmul(left, right):
    return jnp.dot(left, right, preferred_element_type=jnp.float32)

def rope_tables(positions):
    halfway = HEAD_DIM // 2
    inverse = rope_base ** (-2.0 * jnp.arange(halfway, dtype=jnp.float32) / HEAD_DIM)
    angles = positions.astype(jnp.float32)[:, None] * inverse[None, :]
    return (jnp.cos(angles), jnp.sin(angles))

def head_prepare(values, gain_vec, cosine, sine):
    scaling = lax.rsqrt(lax.optimization_barrier(jnp.mean(values * values, axis=-1, keepdims=True)) + epsilon)
    normed = values * scaling * gain_vec
    halfway = HEAD_DIM // 2
    front = normed[..., :halfway]
    back_half = normed[..., halfway:]
    cos_b = cosine[:, None, :]
    sin_b = sine[:, None, :]
    return jnp.concatenate([front * cos_b - back_half * sin_b, back_half * cos_b + front * sin_b], axis=-1)

def visible_keys(positions):
    index_row = jnp.arange(positions.shape[0], dtype=jnp.int32)
    offsets = index_row[:, None] - index_row[None, :]
    return (offsets >= 0) & (offsets <= positions[:, None])

def width_norm(residual):
    rate = lax.rsqrt(lax.optimization_barrier(jnp.mean(residual * residual, axis=-1, keepdims=True)) + epsilon)
    return (residual * rate, rate)

def norm_back(grad_feature, normed, rate, gain_vec, grad_res):
    scaled = grad_feature * gain_vec
    inner = lax.optimization_barrier(jnp.mean(scaled * normed, axis=-1, keepdims=True))
    return (grad_res + rate * (scaled - normed * inner), lax.optimization_barrier(jnp.sum(grad_feature * normed, axis=0)))

def attend(query_h, key_h, value_h, allowed):
    group_size = HEADS // KV_HEADS
    key_full = jnp.repeat(key_h, group_size, axis=1).astype(jnp.float32)
    value_full = jnp.repeat(value_h, group_size, axis=1).astype(jnp.float32)
    scores = jnp.einsum('qhd,khd->hqk', query_h.astype(jnp.float32), key_full) * HEAD_DIM ** (-0.5)
    scores = jnp.where(allowed[None], scores, masked_score)
    top_score = lax.optimization_barrier(jnp.max(scores, axis=-1, keepdims=True))
    log_total = top_score + jnp.log(lax.optimization_barrier(jnp.sum(jnp.exp(scores - top_score), axis=-1, keepdims=True)))
    weights = to_bf16(jnp.exp(scores - log_total)).astype(jnp.float32)
    output = jnp.einsum('hqk,khd->qhd', weights, value_full)
    return (to_bf16(output), log_total)

def attend_back(query_h, key_h, value_h, output_h, log_total, grad_out, allowed):
    group_size = HEADS // KV_HEADS
    scale_factor = HEAD_DIM ** (-0.5)
    key_full = jnp.repeat(key_h, group_size, axis=1).astype(jnp.float32)
    value_full = jnp.repeat(value_h, group_size, axis=1).astype(jnp.float32)
    query_f = query_h.astype(jnp.float32)
    scores = jnp.einsum('qhd,khd->hqk', query_f, key_full) * scale_factor
    scores = jnp.where(allowed[None], scores, masked_score)
    prob_values = jnp.exp(scores - log_total)
    weights = to_bf16(prob_values).astype(jnp.float32)
    grad_f = grad_out.astype(jnp.float32)
    row_inner = lax.optimization_barrier(jnp.sum(grad_f * output_h.astype(jnp.float32), axis=-1))
    grad_value = jnp.einsum('hqk,qhd->khd', weights, grad_f)
    grad_weights = jnp.einsum('qhd,khd->hqk', grad_f, value_full)
    grad_scores = to_bf16(prob_values * (grad_weights - row_inner.T[:, :, None])).astype(jnp.float32)
    grad_query = jnp.einsum('hqk,khd->qhd', grad_scores, key_full) * scale_factor
    grad_key = jnp.einsum('hqk,qhd->khd', grad_scores, query_f) * scale_factor
    seq_length = query_h.shape[0]
    grad_key = grad_key.reshape(seq_length, KV_HEADS, group_size, HEAD_DIM).sum(axis=2)
    grad_value = grad_value.reshape(seq_length, KV_HEADS, group_size, HEAD_DIM).sum(axis=2)
    return (grad_query, grad_key, grad_value)

def sequence_pass(params, hidden_in, positions, grad_out):
    attn_gain, query_weight, key_weight, value_weight, query_gain, key_gain, output_weight, ffn_gain, gate_weight, up_weight, down_weight = params
    cosine, sine = rope_tables(positions)
    allowed = visible_keys(positions)
    seq_length = hidden_in.shape[0]
    residual = hidden_in
    saved = []
    for layer_index in range(LAYERS):
        normed_a, rate_a = width_norm(residual)
        feature_a = to_bf16(normed_a * attn_gain[layer_index])
        query_raw = matmul(feature_a, query_weight[layer_index]).reshape(seq_length, HEADS, HEAD_DIM)
        key_raw = matmul(feature_a, key_weight[layer_index]).reshape(seq_length, KV_HEADS, HEAD_DIM)
        value_raw = matmul(feature_a, value_weight[layer_index]).reshape(seq_length, KV_HEADS, HEAD_DIM)
        query_h = to_bf16(head_prepare(query_raw, query_gain[layer_index], cosine, sine))
        key_h = to_bf16(head_prepare(key_raw, key_gain[layer_index], cosine, sine))
        value_h = to_bf16(value_raw)
        attn_out, log_total = attend(query_h, key_h, value_h, allowed)
        mixed_heads = attn_out.reshape(seq_length, HEADS * HEAD_DIM)
        residual_mid = residual + matmul(mixed_heads, output_weight[layer_index])
        normed_f, rate_f = width_norm(residual_mid)
        feature_f = to_bf16(normed_f * ffn_gain[layer_index])
        gate_value = matmul(feature_f, gate_weight[layer_index])
        up_value = matmul(feature_f, up_weight[layer_index])
        sigmoid_gate = jax.nn.sigmoid(gate_value)
        hidden_act = to_bf16(gate_value * sigmoid_gate * up_value)
        saved.append((normed_a, rate_a, feature_a, query_raw, key_raw, query_h, key_h, value_h, attn_out, log_total, mixed_heads, normed_f, rate_f, feature_f, gate_value, up_value, sigmoid_gate, hidden_act))
        residual = residual_mid + matmul(hidden_act, down_weight[layer_index])
    final_out = residual
    grad_res = grad_out
    layer_grads = [None] * LAYERS
    for layer_index in reversed(range(LAYERS)):
        normed_a, rate_a, feature_a, query_raw, key_raw, query_h, key_h, value_h, attn_out, log_total, mixed_heads, normed_f, rate_f, feature_f, gate_value, up_value, sigmoid_gate, hidden_act = saved[layer_index]
        grad_b = to_bf16(grad_res)
        down_grad = matmul(hidden_act.T, grad_b)
        grad_hidden = matmul(grad_b, down_weight[layer_index].T)
        grad_gate = to_bf16(grad_hidden * up_value * sigmoid_gate * (1.0 + gate_value * (1.0 - sigmoid_gate)))
        grad_up = to_bf16(grad_hidden * gate_value * sigmoid_gate)
        gate_grad = matmul(feature_f.T, grad_gate)
        up_grad = matmul(feature_f.T, grad_up)
        grad_feature = matmul(grad_gate, gate_weight[layer_index].T) + matmul(grad_up, up_weight[layer_index].T)
        grad_res, ffn_gain_grad = norm_back(grad_feature, normed_f, rate_f, ffn_gain[layer_index], grad_res)
        grad_b = to_bf16(grad_res)
        output_grad_w = matmul(mixed_heads.T, grad_b)
        grad_mixed = to_bf16(matmul(grad_b, output_weight[layer_index].T)).reshape(seq_length, HEADS, HEAD_DIM)
        grad_query, grad_key, grad_value = attend_back(query_h, key_h, value_h, attn_out, log_total, grad_mixed, allowed)
        unused_q, query_back = jax.vjp(lambda values, gain_vec: head_prepare(values, gain_vec, cosine, sine), query_raw, query_gain[layer_index])
        grad_query_raw, query_gain_part = query_back(grad_query)
        unused_k, key_back = jax.vjp(lambda values, gain_vec: head_prepare(values, gain_vec, cosine, sine), key_raw, key_gain[layer_index])
        grad_key_raw, key_gain_part = key_back(grad_key)
        query_grad_b = to_bf16(grad_query_raw.reshape(seq_length, HEADS * HEAD_DIM))
        key_grad_b = to_bf16(grad_key_raw.reshape(seq_length, KV_HEADS * HEAD_DIM))
        value_grad_b = to_bf16(grad_value.reshape(seq_length, KV_HEADS * HEAD_DIM))
        query_grad_w = matmul(feature_a.T, query_grad_b)
        key_grad_w = matmul(feature_a.T, key_grad_b)
        value_grad_w = matmul(feature_a.T, value_grad_b)
        grad_feature = matmul(query_grad_b, query_weight[layer_index].T) + matmul(key_grad_b, key_weight[layer_index].T) + matmul(value_grad_b, value_weight[layer_index].T)
        grad_res, attn_gain_grad = norm_back(grad_feature, normed_a, rate_a, attn_gain[layer_index], grad_res)
        layer_grads[layer_index] = (attn_gain_grad, query_grad_w, key_grad_w, value_grad_w, query_gain_part, key_gain_part, output_grad_w, ffn_gain_grad, gate_grad, up_grad, down_grad)
    stacked = tuple((jnp.stack([layer_grads[index][member] for index in range(LAYERS)]) for member in range(11)))
    return (final_out, grad_res, stacked)

def reference(residual_in, positions, attn_gain, query_weight, key_weight, value_weight, query_gain, key_gain, output_weight, ffn_gain, gate_weight, up_weight, down_weight, output_grad):
    params = (attn_gain, query_weight, key_weight, value_weight, query_gain, key_gain, output_weight, ffn_gain, gate_weight, up_weight, down_weight)
    seq_count = residual_in.shape[0] // SEQ_LEN
    stacked_in = residual_in.reshape(seq_count, SEQ_LEN, D)
    stacked_pos = positions.reshape(seq_count, SEQ_LEN)
    stacked_grad = output_grad.reshape(seq_count, SEQ_LEN, D)
    zeros_init = tuple((jnp.zeros(param.shape, jnp.float32) for param in params))

    def scan_step(carry, inputs):
        final_out, grad_in, grads = sequence_pass(params, inputs[0], inputs[1], inputs[2])
        return (tuple((left + right for left, right in zip(carry, grads))), (final_out, grad_in))
    totals, (outputs, input_grads) = lax.scan(scan_step, zeros_init, (stacked_in, stacked_pos, stacked_grad))
    return (outputs.reshape(residual_in.shape[0], D), input_grads.reshape(residual_in.shape[0], D), totals[0], totals[1], totals[2], totals[3], totals[4], totals[5], totals[6], totals[7], totals[8], totals[9], totals[10])
```

```python
import functools

import jax
import jax.numpy as jnp
from jax import lax
from jax.experimental import pallas as pl
from jax.experimental.pallas import tpu as pltpu
from jax.sharding import PartitionSpec as P

HEAD_DIM = 128
LAYERS = 2
SEQ_LEN = 512

epsilon = 1e-06
rope_base = 1000000.0
masked_score = -1e30
MESH = pl.DeviceIdType.MESH
BF = jnp.bfloat16
F32 = jnp.float32


def dot(left, right, dims):
    return lax.dot_general(left, right, (dims, ((), ())), preferred_element_type=F32)


def mm(left, right):
    return dot(left, right, ((1,), (0,)))


def mm_t(left, right):
    return dot(left, right, ((1,), (1,)))


def t_mm(left, right):
    return dot(left, right, ((0,), (0,)))


VM = pl.BlockSpec(memory_space=pltpu.VMEM)


def kernel_id(ids, kind, options, operands):
    key = (kind, options, tuple((array.shape, str(array.dtype)) for array in operands))
    return ids.setdefault(key, len(ids) + 1)


def greet(peers):
    barrier = pltpu.get_barrier_semaphore()
    for peer in peers:
        pl.semaphore_signal(barrier, inc=1, device_id=peer, device_id_type=MESH)
    pl.semaphore_wait(barrier, len(peers))


def block_of(ref, axis, index, size):
    if axis is None:
        return ref
    start = pl.multiple_of(index * size, size)
    where = [slice(None)] * len(ref.shape)
    where[axis] = pl.ds(start, size)
    return ref.at[tuple(where)]


def exchange(arrays, moves, group, ids, after=()):
    names = [name for name, size in group]
    total = 1
    for name, size in group:
        total *= size
    count = len(arrays)
    shapes = []
    for array, (split, concat) in zip(arrays, moves):
        shape = list(array.shape)
        if split is not None:
            shape[split] //= total
        shape[concat] *= total
        shapes.append(jax.ShapeDtypeStruct(tuple(shape), array.dtype))

    extra = len(after)
    collective_id = kernel_id(
        ids, "exchange", (tuple(moves), tuple(group)), (*arrays, *after)
    )

    def kernel(*refs):
        ins, outs = refs[:count], refs[count + extra : 2 * count + extra]
        send, recv, local = refs[2 * count + extra :]
        me = 0
        for name, size in group:
            me = me * size + lax.axis_index(name)

        def coords(index):
            found = {}
            for name, size in reversed(group):
                found[name] = lax.rem(index, size)
                index = index // size
            return found

        others = [lax.rem(me + offset, total) for offset in range(1, total)]
        greet([coords(other) for other in others])
        copies = []
        for which, (split, concat) in enumerate(moves):
            own_size = outs[which].shape[concat] // total
            cut_size = None if split is None else outs[which].shape[split]
            for slot, other in enumerate(others):
                copy = pltpu.make_async_remote_copy(
                    src_ref=block_of(ins[which], split, other, cut_size),
                    dst_ref=block_of(outs[which], concat, me, own_size),
                    send_sem=send.at[which, slot],
                    recv_sem=recv.at[which, slot],
                    device_id=coords(other),
                    device_id_type=MESH,
                )
                copy.start()
                copies.append(copy)
            copy = pltpu.make_async_copy(
                block_of(ins[which], split, me, cut_size),
                block_of(outs[which], concat, me, own_size),
                local.at[which],
            )
            copy.start()
            copies.append(copy)
        for copy in copies:
            copy.wait()

    return pl.pallas_call(
        kernel,
        out_shape=shapes,
        in_specs=[VM] * (count + extra),
        out_specs=[VM] * count,
        scratch_shapes=[
            pltpu.SemaphoreType.DMA((count, total - 1)),
            pltpu.SemaphoreType.DMA((count, total - 1)),
            pltpu.SemaphoreType.DMA((count,)),
        ],
        compiler_params=pltpu.CompilerParams(
            collective_id=collective_id, has_side_effects=True, vmem_limit_bytes=48 << 20
        ),
    )(*arrays, *after)


def line_peers(row, col, rows, cols):
    row_peers = [lax.rem(row + step, rows) for step in range(1, rows)]
    col_peers = [lax.rem(col + step, cols) for step in range(1, cols)]
    return row_peers, col_peers


def gather_tokens(values, rows, cols, ids, after=None):
    size, width = values.shape

    extra = 0 if after is None else 1
    operands = [values] if after is None else [values, after]
    collective_id = kernel_id(ids, "gather", (), operands)

    def kernel(in_ref, *refs):
        out_ref, col_send, col_recv, row_send, row_recv = refs[extra:]
        row, col = lax.axis_index("row"), lax.axis_index("col")
        row_peers, col_peers = line_peers(row, col, rows, cols)
        greet([{"row": peer} for peer in row_peers] + [{"col": peer} for peer in col_peers])

        def place(at_row, at_col):
            start = pl.multiple_of((at_row * cols + at_col) * size, size)
            return out_ref.at[pl.ds(start, size), :]

        copies = []
        for step in range(cols - 1, 0, -1):
            copy = pltpu.make_async_remote_copy(
                src_ref=in_ref,
                dst_ref=place(row, col),
                send_sem=col_send.at[step - 1],
                recv_sem=col_recv.at[step - 1],
                device_id={"col": col_peers[step - 1]},
                device_id_type=MESH,
            )
            copy.start()
            copies.append(copy)

        def to_row(source, target_col, slot):
            for step, peer in enumerate(row_peers):
                copy = pltpu.make_async_remote_copy(
                    src_ref=source,
                    dst_ref=place(row, target_col),
                    send_sem=row_send.at[step, slot],
                    recv_sem=row_recv.at[step, slot],
                    device_id={"row": peer},
                    device_id_type=MESH,
                )
                copy.start()
                rest.append(copy)

        rest = []
        to_row(in_ref, col, 0)
        place(row, col)[...] = in_ref[...]
        for step in range(1, cols):
            copies[cols - 1 - step].wait_recv()
            source_col = lax.rem(col + cols - step, cols)
            to_row(place(row, source_col), source_col, step)
        for copy in copies:
            copy.wait_send()
        for copy in rest:
            copy.wait()

    return pl.pallas_call(
        kernel,
        out_shape=jax.ShapeDtypeStruct((rows * cols * size, width), values.dtype),
        in_specs=[VM] * (1 + extra),
        out_specs=VM,
        scratch_shapes=[
            pltpu.SemaphoreType.DMA((cols - 1,)),
            pltpu.SemaphoreType.DMA((cols - 1,)),
            pltpu.SemaphoreType.DMA((rows - 1, cols)),
            pltpu.SemaphoreType.DMA((rows - 1, cols)),
        ],
        compiler_params=pltpu.CompilerParams(
            collective_id=collective_id, has_side_effects=True
        ),
    )(*operands)


def scatter_tokens(partial, rows, cols, ids, after=None):
    tokens, width = partial.shape
    size = tokens // (rows * cols)

    extra = 0 if after is None else 1
    operands = [partial] if after is None else [partial, after]
    collective_id = kernel_id(ids, "scatter", (), operands)

    def kernel(in_ref, *refs):
        out_ref, got_row, mid, got_col, row_send, row_recv, col_send, col_recv = refs[extra:]
        row, col = lax.axis_index("row"), lax.axis_index("col")
        row_peers, col_peers = line_peers(row, col, rows, cols)
        greet([{"row": peer} for peer in row_peers] + [{"col": peer} for peer in col_peers])

        def place(at_row, at_col):
            start = pl.multiple_of((at_row * cols + at_col) * size, size)
            return in_ref.at[pl.ds(start, size), :]

        order = list(range(1, cols)) + [0]
        first = {}
        for slot in order:
            target = lax.rem(col + slot, cols)
            for step, peer in enumerate(row_peers):
                copy = pltpu.make_async_remote_copy(
                    src_ref=place(peer, target),
                    dst_ref=got_row.at[step, slot],
                    send_sem=row_send.at[step, slot],
                    recv_sem=row_recv.at[step, slot],
                    device_id={"row": peer},
                    device_id_type=MESH,
                )
                copy.start()
                first[step, slot] = copy

        def pair_sum(slot):
            sum_here = place(row, lax.rem(col + slot, cols))[...].astype(F32)
            for step in range(rows - 1):
                first[step, slot].wait_recv()
                sum_here += got_row[step, slot].astype(F32)
            return sum_here

        second = []
        for slot in range(1, cols):
            mid[slot - 1] = pair_sum(slot).astype(mid.dtype)
            copy = pltpu.make_async_remote_copy(
                src_ref=mid.at[slot - 1],
                dst_ref=got_col.at[slot - 1],
                send_sem=col_send.at[slot - 1],
                recv_sem=col_recv.at[slot - 1],
                device_id={"col": col_peers[slot - 1]},
                device_id_type=MESH,
            )
            copy.start()
            second.append(copy)
        out_ref[...] = pair_sum(0)
        for slot in range(1, cols):
            second[slot - 1].wait_recv()
            out_ref[...] += got_col[slot - 1].astype(F32)
        for copy in first.values():
            copy.wait_send()
        for copy in second:
            copy.wait_send()

    return pl.pallas_call(
        kernel,
        out_shape=jax.ShapeDtypeStruct((size, width), F32),
        in_specs=[VM] * (1 + extra),
        out_specs=VM,
        scratch_shapes=[
            pltpu.VMEM((rows - 1, cols, size, width), partial.dtype),
            pltpu.VMEM((cols - 1, size, width), partial.dtype),
            pltpu.VMEM((cols - 1, size, width), partial.dtype),
            pltpu.SemaphoreType.DMA((rows - 1, cols)),
            pltpu.SemaphoreType.DMA((rows - 1, cols)),
            pltpu.SemaphoreType.DMA((cols - 1,)),
            pltpu.SemaphoreType.DMA((cols - 1,)),
        ],
        compiler_params=pltpu.CompilerParams(
            collective_id=collective_id, has_side_effects=True
        ),
    )(*operands)


def half_turn(values):
    return pltpu.roll(values, HEAD_DIM // 2, 1)


def head_norm(values):
    scaling = lax.rsqrt(jnp.mean(values * values, axis=-1, keepdims=True) + epsilon)
    return values * scaling, scaling


def rotate(values, cosine, sine):
    return values * cosine + half_turn(values) * sine


def unrotate(values, cosine, sine):
    return values * cosine + half_turn(values * sine)


def head_prepare(values, gain, cosine, sine):
    normed, scaling = head_norm(values)
    return rotate(normed * gain, cosine, sine).astype(BF)


def head_back(grad, values, gain, cosine, sine):
    normed, scaling = head_norm(values)
    turned = unrotate(grad, cosine, sine)
    scaled = turned * gain
    inner = jnp.mean(scaled * normed, axis=-1, keepdims=True)
    return (
        scaling * (scaled - normed * inner),
        jnp.sum(turned * normed, axis=0, keepdims=True),
    )


def masked_scores(query, key, positions):
    scores = mm_t(query, key) * HEAD_DIM ** (-0.5)
    offsets = lax.broadcasted_iota(jnp.int32, scores.shape, 0) - lax.broadcasted_iota(
        jnp.int32, scores.shape, 1
    )
    allowed = (offsets >= 0) & (offsets <= positions)
    return jnp.where(allowed, scores, masked_score)


def head(ref, seq, index):
    return ref.at[pl.ds(seq * SEQ_LEN, SEQ_LEN), pl.ds(index * HEAD_DIM, HEAD_DIM)]


def seq_rows(ref, seq):
    return ref.at[pl.ds(seq * SEQ_LEN, SEQ_LEN), :]


def attend(query, key, value, gains, cosine, sine, positions):
    tokens, kv_count = query.shape[0], key.shape[1] // HEAD_DIM
    group_size = query.shape[1] // key.shape[1]

    def kernel(q_ref, k_ref, v_ref, gain_ref, cos_ref, sin_ref, pos_ref, out_ref, lse_ref):
        for seq in range(tokens // SEQ_LEN):
            cos_s, sin_s = seq_rows(cos_ref, seq)[...], seq_rows(sin_ref, seq)[...]
            pos_s = seq_rows(pos_ref, seq)[...]
            for kv in range(kv_count):
                key_h = head_prepare(head(k_ref, seq, kv)[...], gain_ref[1:2], cos_s, sin_s)
                value_h = head(v_ref, seq, kv)[...].astype(BF)
                for member in range(group_size):
                    index = kv * group_size + member
                    query_h = head_prepare(
                        head(q_ref, seq, index)[...], gain_ref[0:1], cos_s, sin_s
                    )
                    scores = masked_scores(query_h, key_h, pos_s)
                    top = jnp.max(scores, axis=-1, keepdims=True)
                    lse = top + jnp.log(jnp.sum(jnp.exp(scores - top), axis=-1, keepdims=True))
                    weights = jnp.exp(scores - lse).astype(BF)
                    head(out_ref, seq, index)[...] = mm(weights, value_h).astype(BF)
                    head(lse_ref, seq, index)[...] = jnp.broadcast_to(lse, (SEQ_LEN, HEAD_DIM))

    return pl.pallas_call(
        kernel,
        out_shape=[
            jax.ShapeDtypeStruct(query.shape, BF),
            jax.ShapeDtypeStruct(query.shape, F32),
        ],
        in_specs=[VM] * 7,
        out_specs=[VM] * 2,
        compiler_params=pltpu.CompilerParams(vmem_limit_bytes=40 << 20),
    )(query, key, value, gains, cosine, sine, positions)


def attend_back(query, key, value, gains, cosine, sine, positions, output, lse, grad_out):
    tokens, kv_count = query.shape[0], key.shape[1] // HEAD_DIM
    group_size = query.shape[1] // key.shape[1]
    scale = HEAD_DIM ** (-0.5)

    def kernel(
        q_ref, k_ref, v_ref, gain_ref, cos_ref, sin_ref, pos_ref, out_ref, lse_ref, do_ref,
        dq_ref, dk_ref, dv_ref, dgain_ref,
    ):
        gain_q, gain_k = gain_ref[0:1], gain_ref[1:2]
        total_q = jnp.zeros((1, HEAD_DIM), F32)
        total_k = jnp.zeros((1, HEAD_DIM), F32)
        for seq in range(tokens // SEQ_LEN):
            cos_s, sin_s = seq_rows(cos_ref, seq)[...], seq_rows(sin_ref, seq)[...]
            pos_s = seq_rows(pos_ref, seq)[...]
            for kv in range(kv_count):
                raw_k = head(k_ref, seq, kv)[...]
                key_h = head_prepare(raw_k, gain_k, cos_s, sin_s)
                value_h = head(v_ref, seq, kv)[...].astype(BF)
                grad_k = jnp.zeros((SEQ_LEN, HEAD_DIM), F32)
                grad_v = jnp.zeros((SEQ_LEN, HEAD_DIM), F32)
                for member in range(group_size):
                    index = kv * group_size + member
                    raw_q = head(q_ref, seq, index)[...]
                    query_h = head_prepare(raw_q, gain_q, cos_s, sin_s)
                    scores = masked_scores(query_h, key_h, pos_s)
                    probs = jnp.exp(scores - head(lse_ref, seq, index)[...][:, 0:1])
                    grad_o = head(do_ref, seq, index)[...]
                    inner = jnp.sum(
                        grad_o.astype(F32) * head(out_ref, seq, index)[...].astype(F32),
                        axis=-1,
                        keepdims=True,
                    )
                    grad_v += t_mm(probs.astype(BF), grad_o)
                    grad_s = (probs * (mm_t(grad_o, value_h) - inner)).astype(BF)
                    grad_q = mm(grad_s, key_h) * scale
                    grad_k += t_mm(grad_s, query_h)
                    back_q, part_q = head_back(grad_q, raw_q, gain_q, cos_s, sin_s)
                    head(dq_ref, seq, index)[...] = back_q.astype(BF)
                    total_q += part_q
                back_k, part_k = head_back(grad_k * scale, raw_k, gain_k, cos_s, sin_s)
                head(dk_ref, seq, kv)[...] = back_k.astype(BF)
                head(dv_ref, seq, kv)[...] = grad_v.astype(BF)
                total_k += part_k
        dgain_ref[0:1] = total_q
        dgain_ref[1:2] = total_k

    return pl.pallas_call(
        kernel,
        out_shape=[
            jax.ShapeDtypeStruct(query.shape, BF),
            jax.ShapeDtypeStruct(key.shape, BF),
            jax.ShapeDtypeStruct(value.shape, BF),
            jax.ShapeDtypeStruct(gains.shape, F32),
        ],
        in_specs=[VM] * 10,
        out_specs=[VM] * 4,
        compiler_params=pltpu.CompilerParams(vmem_limit_bytes=40 << 20),
    )(query, key, value, gains, cosine, sine, positions, output, lse, grad_out)


def width_norm(residual):
    rate = lax.rsqrt(jnp.mean(residual * residual, axis=1, keepdims=True) + epsilon)
    return (residual * rate, rate)


def norm_back(grad_feature, normed, rate, gain_vec, grad_res):
    scaled = grad_feature * gain_vec
    inner = jnp.mean(scaled * normed, axis=1, keepdims=True)
    return (
        grad_res + rate * (scaled - normed * inner),
        jnp.sum(grad_feature * normed, axis=0),
    )


def per_device(
    sizes,
    residual_in,
    positions,
    attn_gain,
    query_weight,
    key_weight,
    value_weight,
    query_gain,
    key_gain,
    output_weight,
    ffn_gain,
    gate_weight,
    up_weight,
    down_weight,
    output_grad,
):
    dp_size, rows, cols = sizes
    ids = {}
    group = (("row", rows), ("col", cols))
    pair = (("row", rows),)
    gather = functools.partial(gather_tokens, rows=rows, cols=cols, ids=ids)
    scatter = functools.partial(scatter_tokens, rows=rows, cols=cols, ids=ids)

    halfway = HEAD_DIM // 2
    inverse = rope_base ** (-2.0 * jnp.arange(halfway, dtype=F32) / HEAD_DIM)
    angles = positions.astype(F32)[:, None] * inverse[None, :]
    cosine, sine = jnp.cos(angles), jnp.sin(angles)
    cosine = jnp.concatenate([cosine, cosine], axis=1)
    sine = jnp.concatenate([-sine, sine], axis=1)
    pos_column = positions[:, None]

    residual, grad_res, gains = exchange(
        [residual_in, output_grad, jnp.concatenate([attn_gain, ffn_gain])],
        [(0, 1), (0, 1), (None, 1)],
        group,
        ids,
    )
    attn_gain, ffn_gain = gains[:LAYERS], gains[LAYERS:]
    weights = exchange(
        [
            query_weight,
            key_weight,
            value_weight,
            gate_weight,
            up_weight,
            output_weight,
            down_weight,
        ],
        [(2, 1)] * 5 + [(1, 2)] * 2,
        pair,
        ids,
    )
    query_w, key_w, value_w, gate_w, up_w, output_w, down_w = weights
    head_gains = jnp.stack([query_gain, key_gain], axis=1)

    link = ()

    def corner(array):
        return array[:16, :HEAD_DIM]

    def weight_sums(parts, moves, link):
        joined = exchange(parts, moves, pair, ids, link)
        sums = lax.psum(tuple(joined), "dp")
        return sums, tuple(corner(total) for total in sums), corner(joined[0])

    top_grad = gather(grad_res.astype(BF))
    saved = []
    for layer in range(LAYERS):
        normed_a, rate_a = width_norm(residual)
        feat_a = gather((normed_a * attn_gain[layer]).astype(BF))
        query = mm(feat_a, query_w[layer])
        key = mm(feat_a, key_w[layer])
        value = mm(feat_a, value_w[layer])
        att, lse = attend(query, key, value, head_gains[layer], cosine, sine, pos_column)
        residual_mid = residual + scatter(mm(att, output_w[layer]).astype(BF))
        normed_f, rate_f = width_norm(residual_mid)
        feat_f = gather((normed_f * ffn_gain[layer]).astype(BF))
        gate = mm(feat_f, gate_w[layer])
        up = mm(feat_f, up_w[layer])
        hidden = (gate * jax.nn.sigmoid(gate) * up).astype(BF)
        saved.append(
            (normed_a, rate_a, feat_a, query, key, value, att, lse)
            + (normed_f, rate_f, feat_f, gate, up, hidden)
        )
        joined = None
        if layer == LAYERS - 1:
            down_sums, link, joined = weight_sums(
                [t_mm(hidden, top_grad).astype(BF)], [(1, 0)], link
            )
        residual = residual_mid + scatter(mm(hidden, down_w[layer]).astype(BF), after=joined)

    reduced = [None] * LAYERS
    attn_parts, ffn_parts, head_parts = [None] * LAYERS, [None] * LAYERS, [None] * LAYERS
    for layer in reversed(range(LAYERS)):
        normed_a, rate_a, feat_a, query, key, value, att, lse = saved[layer][:8]
        normed_f, rate_f, feat_f, gate, up, hidden = saved[layer][8:]
        grad_all = top_grad if layer == LAYERS - 1 else gather(
            grad_res.astype(BF), after=joined
        )
        grad_hidden = mm_t(grad_all, down_w[layer])
        sigmoid = jax.nn.sigmoid(gate)
        grad_gate = (grad_hidden * up * sigmoid * (1.0 + gate * (1.0 - sigmoid))).astype(BF)
        grad_up = (grad_hidden * gate * sigmoid).astype(BF)
        grad_feature = scatter(
            (mm_t(grad_gate, gate_w[layer]) + mm_t(grad_up, up_w[layer])).astype(BF)
        )
        link += (corner(grad_feature),)
        ffn_grads = [t_mm(feat_f, grad_gate).astype(BF), t_mm(feat_f, grad_up).astype(BF)]
        if layer == LAYERS - 1:
            ffn_sums, link, joined = weight_sums(ffn_grads, [(0, 1)] * 2, link)
            ffn_sums = tuple(ffn_sums) + tuple(down_sums)
        else:
            ffn_grads.append(t_mm(hidden, grad_all).astype(BF))
            ffn_sums, link, joined = weight_sums(ffn_grads, [(0, 1)] * 2 + [(1, 0)], link)
        grad_res, ffn_parts[layer] = norm_back(
            grad_feature, normed_f, rate_f, ffn_gain[layer], grad_res
        )
        grad_all = gather(grad_res.astype(BF), after=joined)
        grad_att = mm_t(grad_all, output_w[layer]).astype(BF)
        grad_q, grad_k, grad_v, head_parts[layer] = attend_back(
            query, key, value, head_gains[layer], cosine, sine, pos_column, att, lse, grad_att
        )
        grad_feature = scatter(
            (
                mm_t(grad_q, query_w[layer])
                + mm_t(grad_k, key_w[layer])
                + mm_t(grad_v, value_w[layer])
            ).astype(BF)
        )
        link += (corner(grad_feature),)
        attn_sums, link, joined = weight_sums(
            [
                t_mm(feat_a, grad_q).astype(BF),
                t_mm(feat_a, grad_k).astype(BF),
                t_mm(feat_a, grad_v).astype(BF),
                t_mm(att, grad_all).astype(BF),
            ],
            [(0, 1)] * 3 + [(1, 0)],
            link,
        )
        grad_res, attn_parts[layer] = norm_back(
            grad_feature, normed_a, rate_a, attn_gain[layer], grad_res
        )
        reduced[layer] = tuple(attn_sums) + tuple(ffn_sums)

    width_parts = jnp.stack(attn_parts + ffn_parts)
    head_parts = jnp.concatenate(head_parts)
    outputs, input_grad, width_all, head_all = exchange(
        [residual, grad_res, width_parts, head_parts],
        [(1, 0), (1, 0), (1, 0), (None, 0)],
        group,
        ids,
        (joined,),
    )
    small = jnp.concatenate(
        [
            width_all.reshape(rows * cols, -1, width_all.shape[1]).sum(axis=0),
            head_all.reshape(rows * cols, -1, HEAD_DIM).sum(axis=0),
        ]
    )
    (small_all,) = exchange([small], [(None, 0)], (("dp", dp_size),), ids)
    small = small_all.reshape(dp_size, -1, HEAD_DIM).sum(axis=0)
    width_own, head_sum = small[: 2 * LAYERS], small[2 * LAYERS :].reshape(LAYERS, 2, HEAD_DIM)
    stacked = [
        jnp.stack([reduced[layer][member].astype(F32) for layer in range(LAYERS)])
        for member in range(7)
    ]
    return (
        outputs,
        input_grad,
        width_own[:LAYERS],
        stacked[0],
        stacked[1],
        stacked[2],
        head_sum[:, 0],
        head_sum[:, 1],
        stacked[3],
        width_own[LAYERS:],
        stacked[4],
        stacked[5],
        stacked[6],
    )


def solution(mesh):
    wide = P("dp", ("row", "col"))
    gain = P(None, ("row", "col"))
    into, out_of = P(None, "row", "col"), P(None, "col", "row")
    in_specs = (
        wide, P("dp"), gain, into, into, into, P(), P(), out_of, gain, into, into, out_of, wide,
    )
    out_specs = (wide, wide, gain, into, into, into, P(), P(), out_of, gain, into, into, out_of)
    return jax.shard_map(
        functools.partial(per_device, (mesh.shape["dp"], mesh.shape["row"], mesh.shape["col"])),
        mesh=mesh,
        in_specs=in_specs,
        out_specs=out_specs,
        check_vma=False,
    )
```
